32 devices in a mesh: sky: 8 (over z, x), tm: 4 (over y, core).
Axes of the slice: x: 2, y: 2, z: 4, core: 2. Of those that a mesh axis runs over, the one named last changes fastest.
Arguments:
- observed: float32 [4096, 128], P(('sky', 'tm')), may hold values from -12 to 12
- att_partials: bfloat16 [3, 4096, 128], P(None, ('sky', 'tm')), may hold values from -6 to 6
- src_partials: bfloat16 [5, 4096, 128], P(None, ('sky', 'tm')), may hold values from -6 to 6
- src_slot: int32 [4096], P(('sky', 'tm')), may hold values from 0 to 1023
- knot_block: int32 [4096], P(('sky', 'tm')), may hold values from 0 to 255, as said below
- live_count: int32 [32], P(('sky', 'tm')), may hold values from 32 to 128, as said below
- sources: float32 [5, 8192], P(None, 'sky'), may hold values from -6 to 6
- inverses: float32 [5, 5, 8192], P(None, None, 'sky')
- attitude: float32 [3, 4, 4096], P(None, 'tm', 'sky'), may hold values from -6 to 6
- band_coef: float32 [3, 3, 4, 4096], P(None, None, 'tm', 'sky'), may hold values from 0.5 to 4
- extra_diag: float32 [3, 4, 4096], P(None, 'tm', 'sky'), may hold values from 0.05 to 0.5
- band_offsets: int32 [3], replicated, may hold values from 1 to 16, as said below
Outputs:
- sources_out: float32 [5, 8192], P(None, 'sky')
- attitude_out: float32 [3, 4, 4096], P(None, 'tm', 'sky')
The draws below stay inside these ranges and needn't reach their ends.
Inputs may be any that keep to these rules, and one draw needn't show every extreme that they name: On every device, the crossings name blocks of one holder (knot_block // 32) at most 32 times, and some holder exactly 32 times; dead crossings carry blocks too. `live_count`: some device uses all its crossings. `band_offsets`: Distinct; one of them is 16.
All inputs are finite; a program needn't handle non-finite values.
Results may differ from the reference program's by a relative error of at most 0.0003.
Values sent between devices are 32-bit elements; how exact they have to be, the bound alone decides.
A program may use at most 64 MiB of HBM per device.

```python
import math
import jax
import jax.numpy as jnp
from jax import lax

CROSS_DEV = 128
ROWS = 128
BLOCK_KNOTS = 16
SRC_DEV = 1024
NB = 3
HW = 16
SWEEPS = 3
ITERS = 2
BLK_DEV = 32
NBLK = 256
SUBK = 4096
CAP = 32
SOURCES = 8192
CROSSINGS = 4096
N_TM = 4


def draw_knot_block(key, part):
    devices_all = CROSSINGS // CROSS_DEV
    holders = NBLK // BLK_DEV
    slot_total = holders * CAP

    def one_device(device_key):
        key_full, key_score, key_order, key_local = jax.random.split(device_key, 4)
        full_holder = jax.random.randint(key_full, (), 0, holders)
        slot_ids = jnp.arange(slot_total, dtype=jnp.int32)
        scores = jax.random.randint(key_score, (slot_total,), 0, 65536)
        scores = jnp.where(slot_ids // CAP == full_holder, -1, scores)
        ranked = jnp.argsort(scores * slot_total + slot_ids)
        chosen = ranked[:CROSS_DEV] // CAP
        chosen = chosen[jax.random.permutation(key_order, CROSS_DEV)]
        local_blocks = jax.random.randint(key_local, (CROSS_DEV,), 0, BLK_DEV)
        return (chosen * BLK_DEV + local_blocks).astype(jnp.int32)
    keys_all = jax.random.split(jax.random.fold_in(key, 11), devices_all)
    return jax.vmap(one_device)(keys_all).reshape(-1)


def draw_live_count(key, part):
    devices_all = CROSSINGS // CROSS_DEV
    key_div, key_full = jax.random.split(jax.random.fold_in(key, 23))
    divisor = jax.random.randint(key_div, (devices_all,), 1, 5)
    counts = CROSS_DEV // divisor
    full_device = jax.random.randint(key_full, (), 0, devices_all)
    return counts.at[full_device].set(CROSS_DEV).astype(jnp.int32)


def draw_band_offsets(key, part):
    key_pick, key_place = jax.random.split(jax.random.fold_in(key, 37))
    order = jax.random.permutation(key_pick, HW - 1) + 1
    picked = jnp.concatenate([jnp.full((1,), HW, jnp.int32), order[:NB - 1].astype(jnp.int32)])
    placed = jax.random.permutation(key_place, NB)
    return picked[placed].astype(jnp.int32)


def draw_inverses(key, part):
    key_scale, key_noise = jax.random.split(jax.random.fold_in(key, 51))
    scales = jnp.exp(jax.random.uniform(key_scale, (5, SOURCES), jnp.float32, jnp.log(0.001), jnp.log(0.012)))
    noise = 0.2 * jax.random.normal(key_noise, (5, 5, SOURCES), jnp.float32)
    symmetric = 0.5 * (noise + jnp.transpose(noise, (1, 0, 2)))
    identity = jnp.eye(5, dtype=jnp.float32)
    shape_part = identity[:, :, None] + symmetric * (1.0 - identity)[:, :, None]
    return (shape_part * jnp.sqrt(scales[:, None, :] * scales[None, :, :])).astype(jnp.float32)


def place_ends(array, stream_key, low, top_value):
    spot = [jax.random.randint(jax.random.fold_in(stream_key, axis), (), 0, length) for axis, length in enumerate(array.shape)]
    main_axis = array.shape.index(max(array.shape))
    next_to = spot[:main_axis] + [(spot[main_axis] + 1) % array.shape[main_axis]] + spot[main_axis + 1:]
    return array.at[tuple(spot)].set(low).at[tuple(next_to)].set(top_value)


def block_scale(rng, extent, cuts, low, top_value):
    def one(axis_at, blocks):
        heights = jax.random.uniform(jax.random.fold_in(jax.random.fold_in(rng, 6), axis_at), (blocks,), jnp.float32, low / len(cuts), top_value / len(cuts))
        return jnp.repeat(jnp.exp(heights), extent[axis_at] // blocks).reshape((-1,) + (1,) * (len(extent) - axis_at - 1))

    gain = one(*cuts[0])
    for cut in cuts[1:]:
        gain = gain * one(*cut)
    return gain


def bell_draw(rng, shape, deviation, limit, cuts=(), kind=jnp.bfloat16):
    array = deviation * jax.random.normal(rng, shape, jnp.float32)
    if cuts:
        array = array * block_scale(rng, shape, cuts, -0.22, 0.18)
    return jnp.clip(array, -limit, limit).astype(kind)


def setup_inputs(seed: int = 0) -> dict:
    keys = jax.random.split(jax.random.key(seed), 13)
    observed = bell_draw(keys[0], (CROSSINGS, ROWS), 2.0, 12.0, ((0, 32),), jnp.float32)
    att_partials = bell_draw(keys[1], (3, CROSSINGS, ROWS), 1.0, 6.0, ((1, 32),))
    src_partials = bell_draw(keys[2], (5, CROSSINGS, ROWS), 1.0, 6.0, ((1, 32),))
    src_slot = place_ends(jax.random.randint(keys[3], (CROSSINGS,), 0, SRC_DEV), jax.random.fold_in(keys[3], 1), 0, SRC_DEV - 1).astype(jnp.int32)
    knot_block = draw_knot_block(jax.random.fold_in(keys[12], 71), 0)
    live_count = draw_live_count(jax.random.fold_in(keys[12], 71), 0)
    sources = bell_draw(keys[6], (5, SOURCES), 1.0, 6.0, ((1, 8),), jnp.float32)
    inverses = draw_inverses(jax.random.fold_in(keys[12], 71), 0)
    attitude = bell_draw(keys[8], (3, N_TM, SUBK), 1.0, 6.0, ((1, 4), (2, 8)), jnp.float32)
    band_coef = jnp.clip(jnp.exp(math.log(4.0) - 2.0794415 * jax.random.uniform(keys[9], (NB, 3, N_TM, SUBK), jnp.float32) ** block_scale(keys[9], (NB, 3, N_TM, SUBK), ((2, 4), (3, 8)), -0.2, 0.2)), 0.5, 4.0)
    extra_diag = jnp.clip(jnp.exp(math.log(0.5) - 2.3025851 * jax.random.uniform(keys[10], (3, N_TM, SUBK), jnp.float32) ** block_scale(keys[10], (3, N_TM, SUBK), ((1, 4), (2, 8)), -0.2, 0.2)), 0.05, 0.5)
    band_offsets = draw_band_offsets(jax.random.fold_in(keys[12], 71), 0)
    return dict(observed=observed, att_partials=att_partials, src_partials=src_partials, src_slot=src_slot, knot_block=knot_block, live_count=live_count, sources=sources, inverses=inverses, attitude=attitude, band_coef=band_coef, extra_diag=extra_diag, band_offsets=band_offsets)


def spline_table():
    rows_pos = jnp.arange(ROWS, dtype=jnp.float32)
    moments = 1.5 + (BLOCK_KNOTS - 3) * (rows_pos + 0.5) / ROWS
    knot_pos = jnp.arange(BLOCK_KNOTS, dtype=jnp.float32)
    dist = jnp.abs(moments[:, None] - knot_pos[None, :])
    inner = 2.0 / 3.0 - dist * dist + 0.5 * dist * dist * dist
    rest = 2.0 - dist
    outer = rest * rest * rest / 6.0
    return jnp.where(dist < 1.0, inner, jnp.where(dist < 2.0, outer, 0.0))


def source_term(src_partials, values):
    total = jnp.zeros(src_partials.shape[1:], jnp.float32)
    for component in range(5):
        total = total + src_partials[component].astype(jnp.float32) * values[component][:, None]
    return total


def neighbour_sum(field, band_terms, band_offsets, base, length):
    total = jnp.zeros(band_terms.shape[1:], jnp.float32)
    for band_index in range(band_terms.shape[0]):
        offset = band_offsets[band_index].astype(jnp.int32)
        upper = lax.dynamic_slice_in_dim(field, base + offset, length, 1)
        lower = lax.dynamic_slice_in_dim(field, base - offset, length, 1)
        total = total + band_terms[band_index] * (upper + lower)
    return total


def reference(observed, att_partials, src_partials, src_slot, knot_block, live_count, sources, inverses, attitude, band_coef, extra_diag, band_offsets):
    spline = spline_table()
    crossing_count = observed.shape[0]
    position = jnp.arange(crossing_count, dtype=jnp.int32)
    device = position // CROSS_DEV
    sky_block = device // N_TM
    interval = device % N_TM
    live_rows = ((position % CROSS_DEV) < live_count[device]).astype(jnp.float32)[:, None]
    source_index = sky_block * SRC_DEV + src_slot
    block_index = interval * NBLK + knot_block
    knot_total = N_TM * SUBK
    band_terms = band_coef.reshape(NB, 3, knot_total)
    diagonal = extra_diag.reshape(3, knot_total) + 2.0 * jnp.sum(band_terms, axis=0)
    sources_now = sources
    knots_now = attitude.reshape(3, knot_total)
    for outer_step in range(ITERS):
        fetched = jnp.take(knots_now.reshape(3, N_TM * NBLK, BLOCK_KNOTS), block_index, axis=1)
        att_term = jnp.zeros(observed.shape, jnp.float32)
        for axis_index in range(3):
            att_term = att_term + att_partials[axis_index].astype(jnp.float32) * jnp.dot(fetched[axis_index], spline.T, precision=lax.Precision.HIGHEST)
        src_values = jnp.take(sources_now, source_index, axis=1)
        resid = (observed - source_term(src_partials, src_values) - att_term) * live_rows
        rhs = jnp.stack([jnp.sum(src_partials[component].astype(jnp.float32) * resid, axis=1) for component in range(5)])
        normal = jax.ops.segment_sum(rhs.T, source_index, num_segments=SOURCES).T
        step = jnp.einsum("klm,lm->km", inverses, normal, precision=lax.Precision.HIGHEST)
        sources_now = sources_now + step
        resid = resid - live_rows * source_term(src_partials, jnp.take(step, source_index, axis=1))
        grads = jnp.stack([jnp.dot(att_partials[axis_index].astype(jnp.float32) * resid, spline, precision=lax.Precision.HIGHEST) for axis_index in range(3)])
        knot_grad = jnp.stack([jax.ops.segment_sum(grads[axis_index], block_index, num_segments=N_TM * NBLK) for axis_index in range(3)]).reshape(3, knot_total)
        delta = knot_grad / diagonal
        for sweep_index in range(SWEEPS - 1):
            padded = jnp.pad(delta, ((0, 0), (HW, HW)))
            delta = (knot_grad + neighbour_sum(padded, band_terms, band_offsets, HW, knot_total)) / diagonal
        knots_now = knots_now + delta
    return sources_now, knots_now.reshape(3, N_TM, SUBK)
```

```python
import functools

import jax
import jax.numpy as jnp
from jax import lax
from jax.experimental import pallas as pl
from jax.experimental.pallas import tpu as pltpu
from jax.sharding import PartitionSpec as P

BLOCK_KNOTS = 16
SWEEPS = 3
ITERS = 2
NPAR = 5
NAX = 3
LANES = 128
HALO = 8
MESH = pl.DeviceIdType.MESH
F32 = jnp.float32
BF16 = jnp.bfloat16

NN = (((1,), (0,)), ((), ()))
NT = (((1,), (1,)), ((), ()))


def iota(shape, dim):
    return lax.broadcasted_iota(jnp.int32, shape, dim)


def onehot(mask):
    return jnp.where(mask, 1.0, 0.0).astype(BF16)


def parts(x):
    high = x.astype(BF16)
    rest = x - high.astype(F32)
    mid = rest.astype(BF16)
    low = (rest - mid.astype(F32)).astype(BF16)
    return high, mid, low


def mm(a, b, dims):
    return lax.dot_general(a, b, dims, preferred_element_type=F32)


def pick_left(hot, x, dims=NN):
    high, mid, low = parts(x)
    return mm(hot, high, dims) + (mm(hot, mid, dims) + mm(hot, low, dims))


def pick_right(x, hot, dims=NN):
    high, mid, low = parts(x)
    return mm(high, hot, dims) + (mm(mid, hot, dims) + mm(low, hot, dims))


def full_dot(x, y_parts):
    total = None
    x_parts = parts(x)
    for i in (2, 1, 0):
        for j in range(3 - i):
            term = mm(x_parts[i], y_parts[j], NN)
            total = term if total is None else total + term
    return total


def spline_at(row, knot, rows):
    moment = 1.5 + (BLOCK_KNOTS - 3) * (row.astype(F32) + 0.5) / rows
    dist = jnp.abs(moment - knot.astype(F32))
    inner = 2.0 / 3.0 - dist * dist + 0.5 * dist * dist * dist
    rest = 2.0 - dist
    outer = rest * rest * rest / 6.0
    return jnp.where(dist < 1.0, inner, jnp.where(dist < 2.0, outer, 0.0))


def to_blocks(rows, nblocks, fold):
    length = rows[0].shape[1]
    own = (iota((nblocks, length), 1) >> 4) == iota((nblocks, length), 0)
    stacked = jnp.concatenate([jnp.where(own, row, 0.0) for row in rows], axis=0)
    spread = pick_right(stacked, fold)
    lane = iota((nblocks, LANES), 1) >> 4
    out = jnp.zeros((nblocks, LANES), F32)
    for a in range(NAX):
        out = jnp.where(lane == a, spread[a * nblocks : (a + 1) * nblocks], out)
    return out


def kernel(
    n_sky,
    n_tm,
    observed,
    att_partials,
    src_partials,
    src_slot,
    knot_block,
    live_count,
    sources,
    inverses,
    attitude,
    band_coef,
    extra_diag,
    band_offsets,
    sources_out,
    attitude_out,
    knots_all,
    rhs_all,
    grad_mine,
    rim_mine,
    grad_all,
    rim_low,
    rim_high,
    edge_mine,
    edge_near,
    knots_send,
    knots_recv,
    rhs_send,
    rhs_recv,
    grad_send,
    grad_recv,
    rim_send,
    low_recv,
    high_recv,
    edge_send,
    edge_recv,
):
    s = lax.axis_index("sky")
    t = lax.axis_index("tm")
    cross, rows = observed.shape
    knots_here = attitude.shape[2]
    blocks = knots_here // BLOCK_KNOTS
    half = blocks // 2
    span = blocks + 2 * HALO
    span2 = span // 2
    n_blocks = n_sky * blocks
    n_src = sources.shape[1]
    n_band = band_coef.shape[0]

    first_t, last_t = t == 0, t == n_tm - 1
    at_low, at_high = s == 0, s == n_sky - 1
    from_low = jnp.logical_and(at_low, t > 0)
    from_high = jnp.logical_and(at_high, t < n_tm - 1)
    has_left = jnp.logical_not(jnp.logical_and(at_low, first_t))
    has_right = jnp.logical_not(jnp.logical_and(at_high, last_t))
    right = (jnp.where(at_high, 0, s + 1), jnp.where(at_high, jnp.minimum(t + 1, n_tm - 1), t))
    left = (jnp.where(at_low, n_sky - 1, s - 1), jnp.where(at_low, jnp.maximum(t - 1, 0), t))

    barrier = pltpu.get_barrier_semaphore()
    for i in range(1, n_sky):
        pl.semaphore_signal(
            barrier, inc=1, device_id=(lax.rem(s + i, n_sky), t), device_id_type=MESH
        )
    for i in range(1, n_tm):
        pl.semaphore_signal(
            barrier, inc=1, device_id=(s, lax.rem(t + i, n_tm)), device_id_type=MESH
        )

    @pl.when(from_low)
    def _():
        for i in range(n_sky):
            pl.semaphore_signal(barrier, inc=1, device_id=(i, jnp.maximum(t - 1, 0)), device_id_type=MESH)

    @pl.when(from_high)
    def _():
        for i in range(n_sky):
            pl.semaphore_signal(barrier, inc=1, device_id=(i, jnp.minimum(t + 1, n_tm - 1)), device_id_type=MESH)

    def knots_copy(it, i):
        return pltpu.make_async_remote_copy(
            src_ref=knots_all.at[it, s],
            dst_ref=knots_all.at[it, s],
            send_sem=knots_send.at[it, i],
            recv_sem=knots_recv.at[it, i],
            device_id=(lax.rem(s + i, n_sky), t),
            device_id_type=MESH,
        )

    def rhs_copy(it, i):
        return pltpu.make_async_remote_copy(
            src_ref=rhs_all.at[it, t],
            dst_ref=rhs_all.at[it, t],
            send_sem=rhs_send.at[it, i],
            recv_sem=rhs_recv.at[it, i],
            device_id=(s, lax.rem(t + i, n_tm)),
            device_id_type=MESH,
        )

    def grad_copy(it, i):
        to = lax.rem(s + i, n_sky)
        return pltpu.make_async_remote_copy(
            src_ref=grad_mine.at[it, to],
            dst_ref=grad_all.at[it, s],
            send_sem=grad_send.at[it, i],
            recv_sem=grad_recv.at[it, i],
            device_id=(to, t),
            device_id_type=MESH,
        )

    def low_copy(it, sender):
        return pltpu.make_async_remote_copy(
            src_ref=rim_mine.at[it, 0],
            dst_ref=rim_low.at[it, sender],
            send_sem=rim_send.at[it, 0],
            recv_sem=low_recv.at[it, sender],
            device_id=(0, jnp.minimum(t + 1, n_tm - 1)),
            device_id_type=MESH,
        )

    def high_copy(it, sender):
        return pltpu.make_async_remote_copy(
            src_ref=rim_mine.at[it, 1],
            dst_ref=rim_high.at[it, sender],
            send_sem=rim_send.at[it, 1],
            recv_sem=high_recv.at[it, sender],
            device_id=(n_sky - 1, jnp.maximum(t - 1, 0)),
            device_id_type=MESH,
        )

    def edge_copy(side):
        return pltpu.make_async_remote_copy(
            src_ref=edge_mine.at[side],
            dst_ref=edge_near.at[side],
            send_sem=edge_send.at[side],
            recv_sem=edge_recv.at[side],
            device_id=right if side == 0 else left,
            device_id_type=MESH,
        )

    def pack(own):
        return own[:half] + pltpu.roll(own[half:], LANES // 2, 1)

    fold_own = onehot(
        (iota((knots_here, LANES), 0) & 15) == (iota((knots_here, LANES), 1) & 15)
    )
    knots_own = to_blocks([attitude[a] for a in range(NAX)], blocks, fold_own)
    knots_all[0, s] = pack(knots_own)
    lines = [band_coef[b, a] for b in range(n_band) for a in range(NAX)]
    lines = lines + [extra_diag[a] for a in range(NAX)]
    spare = [jnp.zeros((16 - len(lines), LANES), F32)]
    edge_mine[0] = jnp.concatenate([x[:, knots_here - LANES :] for x in lines] + spare, axis=0)
    edge_mine[1] = jnp.concatenate([x[:, :LANES] for x in lines] + spare, axis=0)

    need = (n_sky - 1) + (n_tm - 1) + (t < n_tm - 1).astype(jnp.int32) + (t > 0).astype(jnp.int32)
    pl.semaphore_wait(barrier, need)

    @pl.when(jnp.logical_not(from_low))
    def _():
        rim_low[...] = jnp.zeros(rim_low.shape, F32)

    @pl.when(jnp.logical_not(from_high))
    def _():
        rim_high[...] = jnp.zeros(rim_high.shape, F32)

    for i in range(1, n_sky):
        knots_copy(0, i).start()

    @pl.when(has_right)
    def _():
        edge_copy(0).start()

    @pl.when(has_left)
    def _():
        edge_copy(1).start()

    slot_row = src_slot[...].astype(F32)
    block_row = knot_block[...].astype(F32)
    slot_col = jnp.transpose(jnp.broadcast_to(slot_row, (LANES, cross)))
    block_col = jnp.transpose(jnp.broadcast_to(block_row, (LANES, cross)))
    holder_col = jnp.floor((block_col + 0.5) / blocks)
    local_col = block_col - holder_col * blocks
    upper_col = jnp.where(local_col >= half, 1.0, 0.0)
    place_col = holder_col * half + local_col - upper_col * half

    width = n_sky * half
    knot_hot = onehot(iota((cross, width), 1).astype(F32) == place_col[:, :1])
    lane_upper = jnp.where(iota((cross, LANES), 1) >= LANES // 2, 1.0, 0.0)
    half_mask = lane_upper == upper_col

    gap_rows = jnp.zeros((8 - NPAR, n_src), F32)
    src_list = [x for q in range(NPAR) for x in (inverses[q], gap_rows)]
    src_rows = jnp.concatenate(src_list + [sources[...], gap_rows], axis=0)
    n_rows = src_rows.shape[0]
    src_hot = onehot(iota((cross, n_src), 1).astype(F32) == slot_col[:, :1])
    gathered = pick_left(src_hot, src_rows, NT)

    wide = NPAR * rows
    sel_row = iota((n_rows, wide), 0)
    sel_col = iota((n_rows, wide), 1) // rows
    step_sel = onehot((sel_row >> 3) == sel_col)
    value_sel = onehot(sel_row - NPAR * 8 == sel_col)

    def source_term(spread):
        total = jnp.zeros((cross, rows), F32)
        for p in range(NPAR):
            total = total + src_partials[p].astype(F32) * spread[:, p * rows : (p + 1) * rows]
        return total

    base = observed[...] - source_term(pick_right(gathered, value_sel))
    live = iota((cross, rows), 0) < live_count[0]

    shape = (LANES, NAX * rows)
    c, d = iota(shape, 0) & 63, iota(shape, 1)
    fits = jnp.logical_and((c >> 4) == d // rows, c < NAX * BLOCK_KNOTS)
    look = parts(jnp.where(fits, spline_at(d % rows, c & 15, rows), 0.0))
    shape = (NAX * rows, LANES)
    c, d = iota(shape, 1) & 63, iota(shape, 0)
    fits = jnp.logical_and((c >> 4) == d // rows, c < NAX * BLOCK_KNOTS)
    back = parts(jnp.where(fits, spline_at(d % rows, c & 15, rows), 0.0))

    sum_rows = onehot(iota((16, wide), 0) == iota((16, wide), 1) // rows)

    total_rows = n_sky * span2 + 2 * HALO
    m = iota((total_rows, cross), 0)
    low_target = m - HALO
    high_target = m - HALO + span2
    for h in range(1, n_sky):
        low_target = low_target + jnp.where(m >= h * span2, blocks - span2, 0)
        high_target = high_target + jnp.where(m >= h * span2, blocks - span2, 0)
    extra_row = m - n_sky * span2
    low_target = jnp.where(extra_row >= 0, n_blocks - HALO + extra_row, low_target)
    low_target = jnp.where(extra_row >= HALO, -1, low_target)
    high_target = jnp.where(extra_row >= 0, extra_row - HALO, high_target)
    window_hot = jnp.concatenate(
        [onehot(low_target == knot_block[...]), onehot(high_target == knot_block[...])], axis=1
    )
    lane_low = iota((cross, LANES), 1) < LANES // 2

    shape = (3 * LANES, n_band * LANES)
    c, d = iota(shape, 0), iota(shape, 1)
    from_knot = (c & 15) + ((c >> 7) - 1) * BLOCK_KNOTS
    gap = jnp.abs(from_knot - (d & 15))
    same = jnp.logical_and((c & 127) >> 4 == (d & 127) >> 4, (d & 127) < NAX * BLOCK_KNOTS)
    offset = jnp.zeros(shape, jnp.int32)
    for b in range(n_band):
        offset = jnp.where((d >> 7) == b, band_offsets[b], offset)
    shift_hot = onehot(jnp.logical_and(same, gap == offset))

    for i in range(1, n_sky):
        knots_copy(0, i).wait_recv()

    rhs_total = None
    for it in range(ITERS):
        fetched = pick_left(knot_hot, knots_all[it].reshape(width, LANES))
        fetched = jnp.where(half_mask, fetched, 0.0)
        seen = full_dot(fetched, look)
        att_term = jnp.zeros((cross, rows), F32)
        for a in range(NAX):
            att_term = att_term + att_partials[a].astype(F32) * seen[:, a * rows : (a + 1) * rows]
        resid = jnp.where(live, base - att_term, 0.0)
        weighted = jnp.concatenate(
            [src_partials[p].astype(F32) * resid for p in range(NPAR)], axis=1
        )
        rhs = pick_left(sum_rows, weighted, NT)[:8]
        row = iota((8, cross), 0)
        rhs_all[it, t] = jnp.where(row == NPAR, slot_row, rhs)
        for i in range(1, n_tm):
            rhs_copy(it, i).start()

        if it == 0:
            @pl.when(has_left)
            def _():
                edge_copy(0).wait_recv()

            @pl.when(has_right)
            def _():
                edge_copy(1).wait_recv()

            row = iota((16, LANES), 0)
            blank = jnp.where(
                jnp.logical_and(row >= n_band * NAX, row < (n_band + 1) * NAX), 1.0, 0.0
            )

            @pl.when(jnp.logical_not(has_left))
            def _():
                edge_near[0] = blank

            @pl.when(jnp.logical_not(has_right))
            def _():
                edge_near[1] = blank

            length = knots_here + 2 * LANES
            fold = onehot((iota((length, LANES), 0) & 15) == (iota((length, LANES), 1) & 15))

            near_low, near_high = edge_near[0], edge_near[1]

            def window(at, line):
                return jnp.concatenate(
                    [near_low[at : at + 1], line, near_high[at : at + 1]], axis=1
                )

            bands = [
                to_blocks([window(b * NAX + a, band_coef[b, a]) for a in range(NAX)], span, fold)
                for b in range(n_band)
            ]
            extra = to_blocks(
                [window(n_band * NAX + a, extra_diag[a]) for a in range(NAX)], span, fold
            )
            band_sum = bands[0]
            for b in range(1, n_band):
                band_sum = band_sum + bands[b]
            valid = iota((span, LANES), 1) < NAX * BLOCK_KNOTS
            inv_diag = 1.0 / jnp.where(valid, extra + 2.0 * band_sum, 1.0)

        for i in range(1, n_tm):
            rhs_copy(it, i).wait_recv()
        got = [rhs_all[it, i] for i in range(n_tm)]
        if it == 0:
            same_source = jnp.concatenate(
                [onehot(slot_col == g[NPAR : NPAR + 1]) for g in got], axis=1
            )
            slots_all = jnp.concatenate([g[NPAR : NPAR + 1] for g in got], axis=1)
        rhs_now = jnp.concatenate(got, axis=1)
        rhs_now = jnp.where(iota(rhs_now.shape, 0) < NPAR, rhs_now, 0.0)
        rhs_total = rhs_now if rhs_total is None else rhs_total + rhs_now
        tiled = jnp.concatenate([rhs_now] * NPAR + [jnp.zeros_like(rhs_now)], axis=0)
        normal = pick_left(same_source, tiled, NT)
        moved = source_term(pick_right(gathered * normal, step_sel))
        base = base - moved
        resid = resid - jnp.where(live, moved, 0.0)

        pulled = jnp.concatenate(
            [att_partials[a].astype(F32) * resid for a in range(NAX)], axis=1
        )
        grads = full_dot(pulled, back)
        both = jnp.concatenate(
            [jnp.where(lane_low, grads, 0.0), jnp.where(lane_low, 0.0, grads)], axis=0
        )
        windows = pick_left(window_hot, both)
        grad_mine[it] = windows[: n_sky * span2].reshape(n_sky, span2, LANES)
        rim_mine[it] = windows[n_sky * span2 :].reshape(2, HALO, LANES)
        for i in range(1, n_sky):
            grad_copy(it, i).start()

        @pl.when(t < n_tm - 1)
        def _():
            low_copy(it, s).start()

        @pl.when(t > 0)
        def _():
            high_copy(it, s).start()

        grad_all[it, s] = grad_mine[it, s]

        if it == ITERS - 1:
            full_hot = onehot(
                iota((n_src, n_tm * cross), 0).astype(F32) == slots_all
            )
            padded = jnp.concatenate([rhs_total, jnp.zeros_like(rhs_total)], axis=0)
            normal_all = pick_right(padded, full_hot, NT)[:NPAR]
            steps = [
                jnp.sum(inverses[q] * normal_all, axis=0, keepdims=True) for q in range(NPAR)
            ]
            sources_out[...] = sources[...] + jnp.concatenate(steps, axis=0)

        for i in range(1, n_sky):
            grad_copy(it, i).wait_recv()

        @pl.when(from_low)
        def _():
            for i in range(n_sky):
                low_copy(it, i).wait_recv()

        @pl.when(from_high)
        def _():
            for i in range(n_sky):
                high_copy(it, i).wait_recv()

        packed = grad_all[it, 0]
        for i in range(1, n_sky):
            packed = packed + grad_all[it, i]
        low, high = rim_low[it, 0], rim_high[it, 0]
        for i in range(1, n_sky):
            low, high = low + rim_low[it, i], high + rim_high[it, i]
        packed = jnp.concatenate(
            [packed[:HALO] + low, packed[HALO : span2 - HALO], packed[span2 - HALO :] + high],
            axis=0,
        )
        grad = jnp.concatenate([packed, pltpu.roll(packed, LANES // 2, 1)], axis=0)
        grad = jnp.where(valid, grad, 0.0)
        delta = grad * inv_diag
        for sweep in range(SWEEPS - 1):
            near = jnp.concatenate(
                [pltpu.roll(delta, 1, 0), delta, pltpu.roll(delta, span - 1, 0)], axis=1
            )
            sums = pick_right(near, shift_hot)
            total = grad
            for b in range(n_band):
                total = total + bands[b] * sums[:, b * LANES : (b + 1) * LANES]
            delta = total * inv_diag
        knots_own = knots_own + delta[HALO : HALO + blocks]
        if it < ITERS - 1:
            knots_all[it + 1, s] = pack(knots_own)
            for i in range(1, n_sky):
                knots_copy(it + 1, i).start()
            for i in range(1, n_sky):
                knots_copy(it + 1, i).wait_recv()

    shape = (LANES, knots_here)
    c, d = iota(shape, 0), iota(shape, 1)
    own = (iota((blocks, knots_here), 1) >> 4) == iota((blocks, knots_here), 0)
    for a in range(NAX):
        unfold = onehot(jnp.logical_and((c >> 4) == a, (c & 15) == (d & 15)))
        line = jnp.where(own, pick_right(knots_own, unfold), 0.0)
        attitude_out[a] = jnp.sum(line, axis=0, keepdims=True)

    for it in range(ITERS):
        for i in range(1, n_sky):
            knots_copy(it, i).wait_send()
            grad_copy(it, i).wait_send()
        for i in range(1, n_tm):
            rhs_copy(it, i).wait_send()

        @pl.when(t < n_tm - 1)
        def _():
            low_copy(it, s).wait_send()

        @pl.when(t > 0)
        def _():
            high_copy(it, s).wait_send()

    @pl.when(has_right)
    def _():
        edge_copy(0).wait_send()

    @pl.when(has_left)
    def _():
        edge_copy(1).wait_send()


def per_device(
    observed,
    att_partials,
    src_partials,
    src_slot,
    knot_block,
    live_count,
    sources,
    inverses,
    attitude,
    band_coef,
    extra_diag,
    band_offsets,
):
    n_sky, n_tm = lax.axis_size("sky"), lax.axis_size("tm")
    blocks = attitude.shape[2] // BLOCK_KNOTS
    span2 = (blocks + 2 * HALO) // 2
    vmem = pl.BlockSpec(memory_space=pltpu.VMEM)
    smem = pl.BlockSpec(memory_space=pltpu.SMEM)
    dma = pltpu.SemaphoreType.DMA
    return pl.pallas_call(
        functools.partial(kernel, n_sky, n_tm),
        out_shape=(
            jax.ShapeDtypeStruct(sources.shape, F32),
            jax.ShapeDtypeStruct(attitude.shape, F32),
        ),
        in_specs=[vmem] * 5 + [smem] + [vmem] * 5 + [smem],
        out_specs=(vmem, vmem),
        scratch_shapes=[
            pltpu.VMEM((ITERS, n_sky, blocks // 2, LANES), F32),
            pltpu.VMEM((ITERS, n_tm, 8, src_slot.shape[0]), F32),
            pltpu.VMEM((ITERS, n_sky, span2, LANES), F32),
            pltpu.VMEM((ITERS, 2, HALO, LANES), F32),
            pltpu.VMEM((ITERS, n_sky, span2, LANES), F32),
            pltpu.VMEM((ITERS, n_sky, HALO, LANES), F32),
            pltpu.VMEM((ITERS, n_sky, HALO, LANES), F32),
            pltpu.VMEM((2, 16, LANES), F32),
            pltpu.VMEM((2, 16, LANES), F32),
            dma((ITERS, n_sky)),
            dma((ITERS, n_sky)),
            dma((ITERS, n_tm)),
            dma((ITERS, n_tm)),
            dma((ITERS, n_sky)),
            dma((ITERS, n_sky)),
            dma((ITERS, 2)),
            dma((ITERS, n_sky)),
            dma((ITERS, n_sky)),
            dma((2,)),
            dma((2,)),
        ],
        compiler_params=pltpu.CompilerParams(collective_id=0, has_side_effects=True),
    )(
        observed,
        att_partials,
        src_partials,
        src_slot[None, :],
        knot_block[None, :],
        live_count,
        sources,
        inverses,
        attitude,
        band_coef,
        extra_diag,
        band_offsets,
    )


def solution(mesh):
    placed = (
        P(("sky", "tm"), None),
        P(None, ("sky", "tm"), None),
        P(None, ("sky", "tm"), None),
        P(("sky", "tm")),
        P(("sky", "tm")),
        P(("sky", "tm")),
        P(None, "sky"),
        P(None, None, "sky"),
        P(None, "tm", "sky"),
        P(None, None, "tm", "sky"),
        P(None, "tm", "sky"),
        P(),
    )
    return jax.shard_map(
        per_device,
        mesh=mesh,
        in_specs=placed,
        out_specs=(P(None, "sky"), P(None, "tm", "sky")),
        check_vma=False,
    )
```

```python
import functools

import jax
import jax.numpy as jnp
from jax import lax
from jax.experimental import pallas as pl
from jax.experimental.pallas import tpu as pltpu
from jax.sharding import PartitionSpec as P

BLOCK_KNOTS = 16
SWEEPS = 3
ITERS = 2
NPAR = 5
NAX = 3
LANES = 128
HALO = 8
MESH = pl.DeviceIdType.MESH
F32 = jnp.float32
BF16 = jnp.bfloat16

NN = (((1,), (0,)), ((), ()))
NT = (((1,), (1,)), ((), ()))


def iota(shape, dim):
    return lax.broadcasted_iota(jnp.int32, shape, dim)


def onehot(mask):
    return jnp.where(mask, 1.0, 0.0).astype(BF16)


def parts(x):
    high = x.astype(BF16)
    return high, (x - high.astype(F32)).astype(BF16)


def mm(a, b, dims):
    return lax.dot_general(a, b, dims, preferred_element_type=F32)


def pick_left(hot, x, dims=NN):
    high, low = parts(x)
    return mm(hot, high, dims) + mm(hot, low, dims)


def pick_right(x, hot, dims=NN):
    high, low = parts(x)
    return mm(high, hot, dims) + mm(low, hot, dims)


def full_dot(x, y_parts):
    high, low = parts(x)
    return mm(high, y_parts[0], NN) + (mm(high, y_parts[1], NN) + mm(low, y_parts[0], NN))


def spline_at(row, knot, rows):
    moment = 1.5 + (BLOCK_KNOTS - 3) * (row.astype(F32) + 0.5) / rows
    dist = jnp.abs(moment - knot.astype(F32))
    inner = 2.0 / 3.0 - dist * dist + 0.5 * dist * dist * dist
    rest = 2.0 - dist
    outer = rest * rest * rest / 6.0
    return jnp.where(dist < 1.0, inner, jnp.where(dist < 2.0, outer, 0.0))


def to_blocks(rows, nblocks, fold):
    length = rows[0].shape[1]
    own = (iota((nblocks, length), 1) >> 4) == iota((nblocks, length), 0)
    stacked = jnp.concatenate([jnp.where(own, row, 0.0) for row in rows], axis=0)
    spread = pick_right(stacked, fold)
    lane = iota((nblocks, LANES), 1) >> 4
    out = jnp.zeros((nblocks, LANES), F32)
    for a in range(NAX):
        out = jnp.where(lane == a, spread[a * nblocks : (a + 1) * nblocks], out)
    return out


def kernel(
    n_sky,
    n_tm,
    observed,
    att_partials,
    src_partials,
    src_slot,
    knot_block,
    live_count,
    sources,
    inverses,
    attitude,
    band_coef,
    extra_diag,
    band_offsets,
    sources_out,
    attitude_out,
    knots_all,
    rhs_all,
    grad_mine,
    rim_mine,
    grad_all,
    rim_low,
    rim_high,
    edge_mine,
    edge_near,
    knots_send,
    knots_recv,
    rhs_send,
    rhs_recv,
    grad_send,
    grad_recv,
    rim_send,
    low_recv,
    high_recv,
    edge_send,
    edge_recv,
):
    s = lax.axis_index("sky")
    t = lax.axis_index("tm")
    cross, rows = observed.shape
    knots_here = attitude.shape[2]
    blocks = knots_here // BLOCK_KNOTS
    half = blocks // 2
    span = blocks + 2 * HALO
    span2 = span // 2
    n_blocks = n_sky * blocks
    n_src = sources.shape[1]
    n_band = band_coef.shape[0]

    first_t, last_t = t == 0, t == n_tm - 1
    at_low, at_high = s == 0, s == n_sky - 1
    from_low = jnp.logical_and(at_low, t > 0)
    from_high = jnp.logical_and(at_high, t < n_tm - 1)
    has_left = jnp.logical_not(jnp.logical_and(at_low, first_t))
    has_right = jnp.logical_not(jnp.logical_and(at_high, last_t))
    right = (jnp.where(at_high, 0, s + 1), jnp.where(at_high, jnp.minimum(t + 1, n_tm - 1), t))
    left = (jnp.where(at_low, n_sky - 1, s - 1), jnp.where(at_low, jnp.maximum(t - 1, 0), t))

    barrier = pltpu.get_barrier_semaphore()
    for i in range(1, n_sky):
        pl.semaphore_signal(
            barrier, inc=1, device_id=(lax.rem(s + i, n_sky), t), device_id_type=MESH
        )
    for i in range(1, n_tm):
        pl.semaphore_signal(
            barrier, inc=1, device_id=(s, lax.rem(t + i, n_tm)), device_id_type=MESH
        )

    @pl.when(from_low)
    def _():
        for i in range(n_sky):
            pl.semaphore_signal(barrier, inc=1, device_id=(i, jnp.maximum(t - 1, 0)), device_id_type=MESH)

    @pl.when(from_high)
    def _():
        for i in range(n_sky):
            pl.semaphore_signal(barrier, inc=1, device_id=(i, jnp.minimum(t + 1, n_tm - 1)), device_id_type=MESH)

    def knots_copy(it, i):
        return pltpu.make_async_remote_copy(
            src_ref=knots_all.at[it, s],
            dst_ref=knots_all.at[it, s],
            send_sem=knots_send.at[it, i],
            recv_sem=knots_recv.at[it, i],
            device_id=(lax.rem(s + i, n_sky), t),
            device_id_type=MESH,
        )

    def rhs_copy(it, i):
        return pltpu.make_async_remote_copy(
            src_ref=rhs_all.at[it, t],
            dst_ref=rhs_all.at[it, t],
            send_sem=rhs_send.at[it, i],
            recv_sem=rhs_recv.at[it, i],
            device_id=(s, lax.rem(t + i, n_tm)),
            device_id_type=MESH,
        )

    def grad_copy(it, i):
        to = lax.rem(s + i, n_sky)
        return pltpu.make_async_remote_copy(
            src_ref=grad_mine.at[it, to],
            dst_ref=grad_all.at[it, s],
            send_sem=grad_send.at[it, i],
            recv_sem=grad_recv.at[it, i],
            device_id=(to, t),
            device_id_type=MESH,
        )

    def low_copy(it, sender):
        return pltpu.make_async_remote_copy(
            src_ref=rim_mine.at[it, 0],
            dst_ref=rim_low.at[it, sender],
            send_sem=rim_send.at[it, 0],
            recv_sem=low_recv.at[it, sender],
            device_id=(0, jnp.minimum(t + 1, n_tm - 1)),
            device_id_type=MESH,
        )

    def high_copy(it, sender):
        return pltpu.make_async_remote_copy(
            src_ref=rim_mine.at[it, 1],
            dst_ref=rim_high.at[it, sender],
            send_sem=rim_send.at[it, 1],
            recv_sem=high_recv.at[it, sender],
            device_id=(n_sky - 1, jnp.maximum(t - 1, 0)),
            device_id_type=MESH,
        )

    def edge_copy(side):
        return pltpu.make_async_remote_copy(
            src_ref=edge_mine.at[side],
            dst_ref=edge_near.at[side],
            send_sem=edge_send.at[side],
            recv_sem=edge_recv.at[side],
            device_id=right if side == 0 else left,
            device_id_type=MESH,
        )

    def pack(own):
        return own[:half] + pltpu.roll(own[half:], LANES // 2, 1)

    fold_own = onehot(
        (iota((knots_here, LANES), 0) & 15) == (iota((knots_here, LANES), 1) & 15)
    )
    knots_own = to_blocks([attitude[a] for a in range(NAX)], blocks, fold_own)
    knots_moved = jnp.zeros((blocks, LANES), F32)
    knots_all[0, s] = pack(knots_own)
    lines = [band_coef[b, a] for b in range(n_band) for a in range(NAX)]
    lines = lines + [extra_diag[a] for a in range(NAX)]
    spare = [jnp.zeros((16 - len(lines), LANES), F32)]
    edge_mine[0] = jnp.concatenate([x[:, knots_here - LANES :] for x in lines] + spare, axis=0)
    edge_mine[1] = jnp.concatenate([x[:, :LANES] for x in lines] + spare, axis=0)

    need = (n_sky - 1) + (n_tm - 1) + (t < n_tm - 1).astype(jnp.int32) + (t > 0).astype(jnp.int32)
    pl.semaphore_wait(barrier, need)

    @pl.when(jnp.logical_not(from_low))
    def _():
        rim_low[...] = jnp.zeros(rim_low.shape, F32)

    @pl.when(jnp.logical_not(from_high))
    def _():
        rim_high[...] = jnp.zeros(rim_high.shape, F32)

    for i in range(1, n_sky):
        knots_copy(0, i).start()

    @pl.when(has_right)
    def _():
        edge_copy(0).start()

    @pl.when(has_left)
    def _():
        edge_copy(1).start()

    slot_row = src_slot[...].astype(F32)
    block_row = knot_block[...].astype(F32)
    slot_col = jnp.transpose(jnp.broadcast_to(slot_row, (LANES, cross)))
    block_col = jnp.transpose(jnp.broadcast_to(block_row, (LANES, cross)))
    holder_col = jnp.floor((block_col + 0.5) / blocks)
    local_col = block_col - holder_col * blocks
    upper_col = jnp.where(local_col >= half, 1.0, 0.0)
    place_col = holder_col * half + local_col - upper_col * half

    width = n_sky * half
    knot_hot = onehot(iota((cross, width), 1).astype(F32) == place_col[:, :1])
    lane_upper = jnp.where(iota((cross, LANES), 1) >= LANES // 2, 1.0, 0.0)
    half_mask = lane_upper == upper_col

    gap_rows = jnp.zeros((8 - NPAR, n_src), F32)
    src_list = [x for q in range(NPAR) for x in (inverses[q], gap_rows)]
    src_rows = jnp.concatenate(src_list + [sources[...], gap_rows], axis=0)
    n_rows = src_rows.shape[0]
    src_hot = onehot(iota((cross, n_src), 1).astype(F32) == slot_col[:, :1])
    gathered = pick_left(src_hot, src_rows, NT)

    wide = NPAR * rows
    sel_row = iota((n_rows, wide), 0)
    sel_col = iota((n_rows, wide), 1) // rows
    step_sel = onehot((sel_row >> 3) == sel_col)
    value_sel = onehot(sel_row - NPAR * 8 == sel_col)

    def source_term(spread):
        total = jnp.zeros((cross, rows), F32)
        for p in range(NPAR):
            total = total + src_partials[p].astype(F32) * spread[:, p * rows : (p + 1) * rows]
        return total

    base = observed[...] - source_term(pick_right(gathered, value_sel))
    live = iota((cross, rows), 0) < live_count[0]

    shape = (LANES, NAX * rows)
    c, d = iota(shape, 0) & 63, iota(shape, 1)
    fits = jnp.logical_and((c >> 4) == d // rows, c < NAX * BLOCK_KNOTS)
    look = parts(jnp.where(fits, spline_at(d % rows, c & 15, rows), 0.0))
    shape = (NAX * rows, LANES)
    c, d = iota(shape, 1) & 63, iota(shape, 0)
    fits = jnp.logical_and((c >> 4) == d // rows, c < NAX * BLOCK_KNOTS)
    back = parts(jnp.where(fits, spline_at(d % rows, c & 15, rows), 0.0))

    sum_rows = onehot(iota((16, wide), 0) == iota((16, wide), 1) // rows)

    att = [att_partials[a].astype(F32) for a in range(NAX)]
    cross_terms = []
    for q in range(NPAR):
        param = src_partials[q].astype(F32)
        cross_terms.append(full_dot(jnp.concatenate([x * param for x in att], axis=1), back))

    def against_params(value):
        return [src_partials[p].astype(F32) * value for p in range(NPAR)]

    on_base = against_params(base)
    live_knots = iota((cross, LANES), 0) < live_count[0]

    total_rows = n_sky * span2 + 2 * HALO
    m = iota((total_rows, cross), 0)
    low_target = m - HALO
    high_target = m - HALO + span2
    for h in range(1, n_sky):
        low_target = low_target + jnp.where(m >= h * span2, blocks - span2, 0)
        high_target = high_target + jnp.where(m >= h * span2, blocks - span2, 0)
    extra_row = m - n_sky * span2
    low_target = jnp.where(extra_row >= 0, n_blocks - HALO + extra_row, low_target)
    low_target = jnp.where(extra_row >= HALO, -1, low_target)
    high_target = jnp.where(extra_row >= 0, extra_row - HALO, high_target)
    window_hot = jnp.concatenate(
        [onehot(low_target == knot_block[...]), onehot(high_target == knot_block[...])], axis=1
    )
    lane_low = iota((cross, LANES), 1) < LANES // 2

    shape = (3 * LANES, n_band * LANES)
    c, d = iota(shape, 0), iota(shape, 1)
    from_knot = (c & 15) + ((c >> 7) - 1) * BLOCK_KNOTS
    gap = jnp.abs(from_knot - (d & 15))
    same = jnp.logical_and((c & 127) >> 4 == (d & 127) >> 4, (d & 127) < NAX * BLOCK_KNOTS)
    offset = jnp.zeros(shape, jnp.int32)
    for b in range(n_band):
        offset = jnp.where((d >> 7) == b, band_offsets[b], offset)
    shift_hot = onehot(jnp.logical_and(same, gap == offset))

    for i in range(1, n_sky):
        knots_copy(0, i).wait_recv()

    rhs_total = None
    for it in range(ITERS):
        fetched = pick_left(knot_hot, knots_all[it].reshape(width, LANES))
        fetched = jnp.where(half_mask, fetched, 0.0)
        weighted = jnp.concatenate(
            [
                jnp.where(live, on_base[p] - fetched * cross_terms[p], 0.0)
                for p in range(NPAR)
            ],
            axis=1,
        )
        rhs = pick_left(sum_rows, weighted, NT)[:8]
        row = iota((8, cross), 0)
        rhs_all[it, t] = jnp.where(row == NPAR, slot_row, rhs)
        for i in range(1, n_tm):
            rhs_copy(it, i).start()

        seen = full_dot(fetched, look)
        att_term = jnp.zeros((cross, rows), F32)
        for a in range(NAX):
            att_term = att_term + att[a] * seen[:, a * rows : (a + 1) * rows]
        resid = jnp.where(live, base - att_term, 0.0)
        grads_before = full_dot(jnp.concatenate([x * resid for x in att], axis=1), back)

        if it == 0:
            @pl.when(has_left)
            def _():
                edge_copy(0).wait_recv()

            @pl.when(has_right)
            def _():
                edge_copy(1).wait_recv()

            row = iota((16, LANES), 0)
            blank = jnp.where(
                jnp.logical_and(row >= n_band * NAX, row < (n_band + 1) * NAX), 1.0, 0.0
            )

            @pl.when(jnp.logical_not(has_left))
            def _():
                edge_near[0] = blank

            @pl.when(jnp.logical_not(has_right))
            def _():
                edge_near[1] = blank

            length = knots_here + 2 * LANES
            fold = onehot((iota((length, LANES), 0) & 15) == (iota((length, LANES), 1) & 15))

            near_low, near_high = edge_near[0], edge_near[1]

            def window(at, line):
                return jnp.concatenate(
                    [near_low[at : at + 1], line, near_high[at : at + 1]], axis=1
                )

            bands = [
                to_blocks([window(b * NAX + a, band_coef[b, a]) for a in range(NAX)], span, fold)
                for b in range(n_band)
            ]
            extra = to_blocks(
                [window(n_band * NAX + a, extra_diag[a]) for a in range(NAX)], span, fold
            )
            band_sum = bands[0]
            for b in range(1, n_band):
                band_sum = band_sum + bands[b]
            valid = iota((span, LANES), 1) < NAX * BLOCK_KNOTS
            inv_diag = 1.0 / jnp.where(valid, extra + 2.0 * band_sum, 1.0)

        for i in range(1, n_tm):
            rhs_copy(it, i).wait_recv()
        got = [rhs_all[it, i] for i in range(n_tm)]
        if it == 0:
            same_source = jnp.concatenate(
                [onehot(slot_col == g[NPAR : NPAR + 1]) for g in got], axis=1
            )
            slots_all = jnp.concatenate([g[NPAR : NPAR + 1] for g in got], axis=1)
        rhs_now = jnp.concatenate(got, axis=1)
        rhs_now = jnp.where(iota(rhs_now.shape, 0) < NPAR, rhs_now, 0.0)
        rhs_total = rhs_now if rhs_total is None else rhs_total + rhs_now
        tiled = jnp.concatenate([rhs_now] * NPAR + [jnp.zeros_like(rhs_now)], axis=0)
        normal = pick_left(same_source, tiled, NT)
        step = pick_right(gathered * normal, step_sel)
        grads_moved = jnp.zeros((cross, LANES), F32)
        for q in range(NPAR):
            grads_moved = grads_moved + step[:, q * rows : (q + 1) * rows] * cross_terms[q]
        grads = grads_before - jnp.where(live_knots, grads_moved, 0.0)
        both = jnp.concatenate(
            [jnp.where(lane_low, grads, 0.0), jnp.where(lane_low, 0.0, grads)], axis=0
        )
        windows = pick_left(window_hot, both)
        grad_mine[it] = windows[: n_sky * span2].reshape(n_sky, span2, LANES)
        rim_mine[it] = windows[n_sky * span2 :].reshape(2, HALO, LANES)
        @pl.when(t < n_tm - 1)
        def _():
            low_copy(it, s).start()

        @pl.when(t > 0)
        def _():
            high_copy(it, s).start()

        for i in range(1, n_sky):
            grad_copy(it, i).start()

        grad_all[it, s] = grad_mine[it, s]

        if it < ITERS - 1:
            base = base - source_term(step)
            on_base = against_params(base)
        if it == ITERS - 1:
            full_hot = onehot(
                iota((n_src, n_tm * cross), 0).astype(F32) == slots_all
            )
            padded = jnp.concatenate([rhs_total, jnp.zeros_like(rhs_total)], axis=0)
            normal_all = pick_right(padded, full_hot, NT)[:NPAR]
            steps = [
                jnp.sum(inverses[q] * normal_all, axis=0, keepdims=True) for q in range(NPAR)
            ]
            sources_out[...] = sources[...] + jnp.concatenate(steps, axis=0)

        for i in range(1, n_sky):
            grad_copy(it, i).wait_recv()

        @pl.when(from_low)
        def _():
            for i in range(n_sky):
                low_copy(it, i).wait_recv()

        @pl.when(from_high)
        def _():
            for i in range(n_sky):
                high_copy(it, i).wait_recv()

        packed = grad_all[it, 0]
        for i in range(1, n_sky):
            packed = packed + grad_all[it, i]
        low, high = rim_low[it, 0], rim_high[it, 0]
        for i in range(1, n_sky):
            low, high = low + rim_low[it, i], high + rim_high[it, i]
        packed = jnp.concatenate(
            [packed[:HALO] + low, packed[HALO : span2 - HALO], packed[span2 - HALO :] + high],
            axis=0,
        )
        grad = jnp.concatenate([packed, pltpu.roll(packed, LANES // 2, 1)], axis=0)
        grad = jnp.where(valid, grad, 0.0)
        delta = grad * inv_diag
        for sweep in range(SWEEPS - 1):
            near = jnp.concatenate(
                [pltpu.roll(delta, 1, 0), delta, pltpu.roll(delta, span - 1, 0)], axis=1
            )
            sums = pick_right(near, shift_hot)
            total = grad
            for b in range(n_band):
                total = total + bands[b] * sums[:, b * LANES : (b + 1) * LANES]
            delta = total * inv_diag
        knots_moved = knots_moved + delta[HALO : HALO + blocks]
        if it < ITERS - 1:
            knots_all[it + 1, s] = pack(knots_own + knots_moved)
            for i in range(1, n_sky):
                knots_copy(it + 1, i).start()
            for i in range(1, n_sky):
                knots_copy(it + 1, i).wait_recv()

    shape = (LANES, knots_here)
    c, d = iota(shape, 0), iota(shape, 1)
    own = (iota((blocks, knots_here), 1) >> 4) == iota((blocks, knots_here), 0)
    for a in range(NAX):
        unfold = onehot(jnp.logical_and((c >> 4) == a, (c & 15) == (d & 15)))
        line = jnp.where(own, pick_right(knots_moved, unfold), 0.0)
        attitude_out[a] = attitude[a] + jnp.sum(line, axis=0, keepdims=True)

    for it in range(ITERS):
        for i in range(1, n_sky):
            knots_copy(it, i).wait_send()
            grad_copy(it, i).wait_send()
        for i in range(1, n_tm):
            rhs_copy(it, i).wait_send()

        @pl.when(t < n_tm - 1)
        def _():
            low_copy(it, s).wait_send()

        @pl.when(t > 0)
        def _():
            high_copy(it, s).wait_send()

    @pl.when(has_right)
    def _():
        edge_copy(0).wait_send()

    @pl.when(has_left)
    def _():
        edge_copy(1).wait_send()


def per_device(
    observed,
    att_partials,
    src_partials,
    src_slot,
    knot_block,
    live_count,
    sources,
    inverses,
    attitude,
    band_coef,
    extra_diag,
    band_offsets,
):
    n_sky, n_tm = lax.axis_size("sky"), lax.axis_size("tm")
    blocks = attitude.shape[2] // BLOCK_KNOTS
    span2 = (blocks + 2 * HALO) // 2
    vmem = pl.BlockSpec(memory_space=pltpu.VMEM)
    smem = pl.BlockSpec(memory_space=pltpu.SMEM)
    dma = pltpu.SemaphoreType.DMA
    return pl.pallas_call(
        functools.partial(kernel, n_sky, n_tm),
        out_shape=(
            jax.ShapeDtypeStruct(sources.shape, F32),
            jax.ShapeDtypeStruct(attitude.shape, F32),
        ),
        in_specs=[vmem] * 5 + [smem] + [vmem] * 5 + [smem],
        out_specs=(vmem, vmem),
        scratch_shapes=[
            pltpu.VMEM((ITERS, n_sky, blocks // 2, LANES), F32),
            pltpu.VMEM((ITERS, n_tm, 8, src_slot.shape[0]), F32),
            pltpu.VMEM((ITERS, n_sky, span2, LANES), F32),
            pltpu.VMEM((ITERS, 2, HALO, LANES), F32),
            pltpu.VMEM((ITERS, n_sky, span2, LANES), F32),
            pltpu.VMEM((ITERS, n_sky, HALO, LANES), F32),
            pltpu.VMEM((ITERS, n_sky, HALO, LANES), F32),
            pltpu.VMEM((2, 16, LANES), F32),
            pltpu.VMEM((2, 16, LANES), F32),
            dma((ITERS, n_sky)),
            dma((ITERS, n_sky)),
            dma((ITERS, n_tm)),
            dma((ITERS, n_tm)),
            dma((ITERS, n_sky)),
            dma((ITERS, n_sky)),
            dma((ITERS, 2)),
            dma((ITERS, n_sky)),
            dma((ITERS, n_sky)),
            dma((2,)),
            dma((2,)),
        ],
        compiler_params=pltpu.CompilerParams(collective_id=0, has_side_effects=True),
    )(
        observed,
        att_partials,
        src_partials,
        src_slot[None, :],
        knot_block[None, :],
        live_count,
        sources,
        inverses,
        attitude,
        band_coef,
        extra_diag,
        band_offsets,
    )


def solution(mesh):
    placed = (
        P(("sky", "tm"), None),
        P(None, ("sky", "tm"), None),
        P(None, ("sky", "tm"), None),
        P(("sky", "tm")),
        P(("sky", "tm")),
        P(("sky", "tm")),
        P(None, "sky"),
        P(None, None, "sky"),
        P(None, "tm", "sky"),
        P(None, None, "tm", "sky"),
        P(None, "tm", "sky"),
        P(),
    )
    return jax.shard_map(
        per_device,
        mesh=mesh,
        in_specs=placed,
        out_specs=(P(None, "sky"), P(None, "tm", "sky")),
        check_vma=False,
    )
```

```python
import functools

import jax
import jax.numpy as jnp
from jax import lax
from jax.experimental import pallas as pl
from jax.experimental.pallas import tpu as pltpu
from jax.sharding import PartitionSpec as P

BLOCK_KNOTS = 16
SWEEPS = 3
ITERS = 2
NPAR = 5
NAX = 3
LANES = 128
HALO = 8
MESH = pl.DeviceIdType.MESH
F32 = jnp.float32
BF16 = jnp.bfloat16

NN = (((1,), (0,)), ((), ()))
NT = (((1,), (1,)), ((), ()))


def iota(shape, dim):
    return lax.broadcasted_iota(jnp.int32, shape, dim)


def onehot(mask):
    return jnp.where(mask, 1.0, 0.0).astype(BF16)


def parts(x):
    high = x.astype(BF16)
    return high, (x - high.astype(F32)).astype(BF16)


def mm(a, b, dims):
    return lax.dot_general(a, b, dims, preferred_element_type=F32)


def pick_left(hot, x, dims=NN):
    high, low = parts(x)
    return mm(hot, high, dims) + mm(hot, low, dims)


def pick_right(x, hot, dims=NN):
    high, low = parts(x)
    return mm(high, hot, dims) + mm(low, hot, dims)


def full_dot(x, y_parts):
    high, low = parts(x)
    return mm(high, y_parts[0], NN) + (mm(high, y_parts[1], NN) + mm(low, y_parts[0], NN))


def spline_at(row, knot, rows):
    moment = 1.5 + (BLOCK_KNOTS - 3) * (row.astype(F32) + 0.5) / rows
    dist = jnp.abs(moment - knot.astype(F32))
    inner = 2.0 / 3.0 - dist * dist + 0.5 * dist * dist * dist
    rest = 2.0 - dist
    outer = rest * rest * rest / 6.0
    return jnp.where(dist < 1.0, inner, jnp.where(dist < 2.0, outer, 0.0))


def to_blocks(rows, nblocks, fold):
    length = rows[0].shape[1]
    own = (iota((nblocks, length), 1) >> 4) == iota((nblocks, length), 0)
    stacked = jnp.concatenate([jnp.where(own, row, 0.0) for row in rows], axis=0)
    spread = pick_right(stacked, fold)
    lane = iota((nblocks, LANES), 1) >> 4
    out = jnp.zeros((nblocks, LANES), F32)
    for a in range(NAX):
        out = jnp.where(lane == a, spread[a * nblocks : (a + 1) * nblocks], out)
    return out


def kernel(
    n_sky,
    n_tm,
    observed,
    att_partials,
    src_partials,
    src_slot,
    knot_block,
    live_count,
    sources,
    inverses,
    attitude,
    band_coef,
    extra_diag,
    band_offsets,
    sources_out,
    attitude_out,
    knots_all,
    rhs_all,
    grad_mine,
    rim_mine,
    grad_all,
    rim_low,
    rim_high,
    edge_mine,
    edge_near,
    knots_send,
    knots_recv,
    rhs_send,
    rhs_recv,
    grad_send,
    grad_recv,
    rim_send,
    low_recv,
    high_recv,
    edge_send,
    edge_recv,
):
    s = lax.axis_index("sky")
    t = lax.axis_index("tm")
    cross, rows = observed.shape
    knots_here = attitude.shape[2]
    blocks = knots_here // BLOCK_KNOTS
    half = blocks // 2
    span = blocks + 2 * HALO
    span2 = span // 2
    n_blocks = n_sky * blocks
    n_src = sources.shape[1]
    n_band = band_coef.shape[0]

    first_t, last_t = t == 0, t == n_tm - 1
    at_low, at_high = s == 0, s == n_sky - 1
    from_low = jnp.logical_and(at_low, t > 0)
    from_high = jnp.logical_and(at_high, t < n_tm - 1)
    has_left = jnp.logical_not(jnp.logical_and(at_low, first_t))
    has_right = jnp.logical_not(jnp.logical_and(at_high, last_t))
    right = (jnp.where(at_high, 0, s + 1), jnp.where(at_high, jnp.minimum(t + 1, n_tm - 1), t))
    left = (jnp.where(at_low, n_sky - 1, s - 1), jnp.where(at_low, jnp.maximum(t - 1, 0), t))

    barrier = pltpu.get_barrier_semaphore()
    for i in range(1, n_sky):
        pl.semaphore_signal(
            barrier, inc=1, device_id=(lax.rem(s + i, n_sky), t), device_id_type=MESH
        )
    for i in range(1, n_tm):
        pl.semaphore_signal(
            barrier, inc=1, device_id=(s, lax.rem(t + i, n_tm)), device_id_type=MESH
        )

    @pl.when(from_low)
    def _():
        for i in range(n_sky):
            pl.semaphore_signal(barrier, inc=1, device_id=(i, jnp.maximum(t - 1, 0)), device_id_type=MESH)

    @pl.when(from_high)
    def _():
        for i in range(n_sky):
            pl.semaphore_signal(barrier, inc=1, device_id=(i, jnp.minimum(t + 1, n_tm - 1)), device_id_type=MESH)

    def knots_copy(it, i):
        return pltpu.make_async_remote_copy(
            src_ref=knots_all.at[it, s],
            dst_ref=knots_all.at[it, s],
            send_sem=knots_send.at[it, i],
            recv_sem=knots_recv.at[it, i],
            device_id=(lax.rem(s + i, n_sky), t),
            device_id_type=MESH,
        )

    def rhs_copy(it, i):
        return pltpu.make_async_remote_copy(
            src_ref=rhs_all.at[it, t],
            dst_ref=rhs_all.at[it, t],
            send_sem=rhs_send.at[it, i],
            recv_sem=rhs_recv.at[it, i],
            device_id=(s, lax.rem(t + i, n_tm)),
            device_id_type=MESH,
        )

    def grad_copy(it, i):
        to = lax.rem(s + i, n_sky)
        return pltpu.make_async_remote_copy(
            src_ref=grad_mine.at[it, to],
            dst_ref=grad_all.at[it, s],
            send_sem=grad_send.at[it, i],
            recv_sem=grad_recv.at[it, i],
            device_id=(to, t),
            device_id_type=MESH,
        )

    def low_copy(it, sender):
        return pltpu.make_async_remote_copy(
            src_ref=rim_mine.at[it, 0],
            dst_ref=rim_low.at[it, sender],
            send_sem=rim_send.at[it, 0],
            recv_sem=low_recv.at[it, sender],
            device_id=(0, jnp.minimum(t + 1, n_tm - 1)),
            device_id_type=MESH,
        )

    def high_copy(it, sender):
        return pltpu.make_async_remote_copy(
            src_ref=rim_mine.at[it, 1],
            dst_ref=rim_high.at[it, sender],
            send_sem=rim_send.at[it, 1],
            recv_sem=high_recv.at[it, sender],
            device_id=(n_sky - 1, jnp.maximum(t - 1, 0)),
            device_id_type=MESH,
        )

    def edge_copy(side):
        return pltpu.make_async_remote_copy(
            src_ref=edge_mine.at[side],
            dst_ref=edge_near.at[side],
            send_sem=edge_send.at[side],
            recv_sem=edge_recv.at[side],
            device_id=right if side == 0 else left,
            device_id_type=MESH,
        )

    def pack(own):
        return own[:half] + pltpu.roll(own[half:], LANES // 2, 1)

    fold_own = onehot(
        (iota((knots_here, LANES), 0) & 15) == (iota((knots_here, LANES), 1) & 15)
    )
    knots_own = to_blocks([attitude[a] for a in range(NAX)], blocks, fold_own)
    knots_moved = jnp.zeros((blocks, LANES), F32)
    knots_all[0, s] = pack(knots_own)
    lines = [band_coef[b, a] for b in range(n_band) for a in range(NAX)]
    lines = lines + [extra_diag[a] for a in range(NAX)]
    spare = [jnp.zeros((16 - len(lines), LANES), F32)]
    edge_mine[0] = jnp.concatenate([x[:, knots_here - LANES :] for x in lines] + spare, axis=0)
    edge_mine[1] = jnp.concatenate([x[:, :LANES] for x in lines] + spare, axis=0)

    need = (n_sky - 1) + (n_tm - 1) + (t < n_tm - 1).astype(jnp.int32) + (t > 0).astype(jnp.int32)
    pl.semaphore_wait(barrier, need)

    @pl.when(jnp.logical_not(from_low))
    def _():
        rim_low[...] = jnp.zeros(rim_low.shape, F32)

    @pl.when(jnp.logical_not(from_high))
    def _():
        rim_high[...] = jnp.zeros(rim_high.shape, F32)

    for i in range(1, n_sky):
        knots_copy(0, i).start()

    @pl.when(has_right)
    def _():
        edge_copy(0).start()

    @pl.when(has_left)
    def _():
        edge_copy(1).start()

    slot_row = src_slot[...].astype(F32)
    block_row = knot_block[...].astype(F32)
    slot_col = jnp.transpose(jnp.broadcast_to(slot_row, (LANES, cross)))
    block_col = jnp.transpose(jnp.broadcast_to(block_row, (LANES, cross)))
    holder_col = jnp.floor((block_col + 0.5) / blocks)
    local_col = block_col - holder_col * blocks
    upper_col = jnp.where(local_col >= half, 1.0, 0.0)
    place_col = holder_col * half + local_col - upper_col * half

    width = n_sky * half
    knot_hot = onehot(iota((cross, width), 1).astype(F32) == place_col[:, :1])
    lane_upper = jnp.where(iota((cross, LANES), 1) >= LANES // 2, 1.0, 0.0)
    half_mask = lane_upper == upper_col

    gap_rows = jnp.zeros((8 - NPAR, n_src), F32)
    src_list = [x for q in range(NPAR) for x in (inverses[q], gap_rows)]
    src_rows = jnp.concatenate(src_list + [sources[...], gap_rows], axis=0)
    n_rows = src_rows.shape[0]
    src_hot = onehot(iota((cross, n_src), 1).astype(F32) == slot_col[:, :1])
    gathered = pick_left(src_hot, src_rows, NT)

    wide = NPAR * rows
    sel_row = iota((n_rows, wide), 0)
    sel_col = iota((n_rows, wide), 1) // rows
    step_sel = onehot((sel_row >> 3) == sel_col)
    value_sel = onehot(sel_row - NPAR * 8 == sel_col)

    def source_term(spread):
        total = jnp.zeros((cross, rows), F32)
        for p in range(NPAR):
            total = total + src_partials[p].astype(F32) * spread[:, p * rows : (p + 1) * rows]
        return total

    base = observed[...] - source_term(pick_right(gathered, value_sel))
    live = iota((cross, rows), 0) < live_count[0]

    shape = (LANES, NAX * rows)
    c, d = iota(shape, 0) & 63, iota(shape, 1)
    fits = jnp.logical_and((c >> 4) == d // rows, c < NAX * BLOCK_KNOTS)
    look = parts(jnp.where(fits, spline_at(d % rows, c & 15, rows), 0.0))
    shape = (NAX * rows, LANES)
    c, d = iota(shape, 1) & 63, iota(shape, 0)
    fits = jnp.logical_and((c >> 4) == d // rows, c < NAX * BLOCK_KNOTS)
    back = parts(jnp.where(fits, spline_at(d % rows, c & 15, rows), 0.0))

    sum_rows = onehot(iota((16, wide), 0) == iota((16, wide), 1) // rows)

    att = [att_partials[a].astype(F32) for a in range(NAX)]
    cross_terms = []
    for q in range(NPAR):
        param = src_partials[q].astype(F32)
        cross_terms.append(full_dot(jnp.concatenate([x * param for x in att], axis=1), back))

    def against_params(value):
        return [src_partials[p].astype(F32) * value for p in range(NPAR)]

    on_base = against_params(base)
    live_knots = iota((cross, LANES), 0) < live_count[0]

    total_rows = n_sky * span2 + 2 * HALO
    m = iota((total_rows, cross), 0)
    low_target = m - HALO
    high_target = m - HALO + span2
    for h in range(1, n_sky):
        low_target = low_target + jnp.where(m >= h * span2, blocks - span2, 0)
        high_target = high_target + jnp.where(m >= h * span2, blocks - span2, 0)
    extra_row = m - n_sky * span2
    low_target = jnp.where(extra_row >= 0, n_blocks - HALO + extra_row, low_target)
    low_target = jnp.where(extra_row >= HALO, -1, low_target)
    high_target = jnp.where(extra_row >= 0, extra_row - HALO, high_target)
    window_hot = jnp.concatenate(
        [onehot(low_target == knot_block[...]), onehot(high_target == knot_block[...])], axis=1
    )
    lane_low = iota((cross, LANES), 1) < LANES // 2

    shape = (3 * LANES, n_band * LANES)
    c, d = iota(shape, 0), iota(shape, 1)
    from_knot = (c & 15) + ((c >> 7) - 1) * BLOCK_KNOTS
    gap = jnp.abs(from_knot - (d & 15))
    same = jnp.logical_and((c & 127) >> 4 == (d & 127) >> 4, (d & 127) < NAX * BLOCK_KNOTS)
    offset = jnp.zeros(shape, jnp.int32)
    for b in range(n_band):
        offset = jnp.where((d >> 7) == b, band_offsets[b], offset)
    shift_hot = onehot(jnp.logical_and(same, gap == offset))

    for i in range(1, n_sky):
        knots_copy(0, i).wait_recv()

    rhs_total = None
    for it in range(ITERS):
        fetched = pick_left(knot_hot, knots_all[it].reshape(width, LANES))
        fetched = jnp.where(half_mask, fetched, 0.0)
        weighted = jnp.concatenate(
            [
                jnp.where(live, on_base[p] - fetched * cross_terms[p], 0.0)
                for p in range(NPAR)
            ],
            axis=1,
        )
        rhs = pick_left(sum_rows, weighted, NT)[:8]
        row = iota((8, cross), 0)
        rhs_all[it, t] = jnp.where(row == NPAR, slot_row, rhs)
        for i in range(1, n_tm):
            rhs_copy(it, i).start()

        seen = full_dot(fetched, look)
        att_term = jnp.zeros((cross, rows), F32)
        for a in range(NAX):
            att_term = att_term + att[a] * seen[:, a * rows : (a + 1) * rows]
        resid = jnp.where(live, base - att_term, 0.0)
        grads_before = full_dot(jnp.concatenate([x * resid for x in att], axis=1), back)

        if it == 0:
            @pl.when(has_left)
            def _():
                edge_copy(0).wait_recv()

            @pl.when(has_right)
            def _():
                edge_copy(1).wait_recv()

            row = iota((16, LANES), 0)
            blank = jnp.where(
                jnp.logical_and(row >= n_band * NAX, row < (n_band + 1) * NAX), 1.0, 0.0
            )

            @pl.when(jnp.logical_not(has_left))
            def _():
                edge_near[0] = blank

            @pl.when(jnp.logical_not(has_right))
            def _():
                edge_near[1] = blank

            length = knots_here + 2 * LANES
            fold = onehot((iota((length, LANES), 0) & 15) == (iota((length, LANES), 1) & 15))

            near_low, near_high = edge_near[0], edge_near[1]

            def window(at, line):
                return jnp.concatenate(
                    [near_low[at : at + 1], line, near_high[at : at + 1]], axis=1
                )

            bands = [
                to_blocks([window(b * NAX + a, band_coef[b, a]) for a in range(NAX)], span, fold)
                for b in range(n_band)
            ]
            extra = to_blocks(
                [window(n_band * NAX + a, extra_diag[a]) for a in range(NAX)], span, fold
            )
            band_sum = bands[0]
            for b in range(1, n_band):
                band_sum = band_sum + bands[b]
            valid = iota((span, LANES), 1) < NAX * BLOCK_KNOTS
            inv_diag = 1.0 / jnp.where(valid, extra + 2.0 * band_sum, 1.0)

        for i in range(1, n_tm):
            rhs_copy(it, i).wait_recv()
        got = [rhs_all[it, i] for i in range(n_tm)]
        if it == 0:
            same_source = jnp.concatenate(
                [onehot(slot_col == g[NPAR : NPAR + 1]) for g in got], axis=1
            )
            slots_all = jnp.concatenate([g[NPAR : NPAR + 1] for g in got], axis=1)
        rhs_now = jnp.concatenate(got, axis=1)
        rhs_now = jnp.where(iota(rhs_now.shape, 0) < NPAR, rhs_now, 0.0)
        rhs_total = rhs_now if rhs_total is None else rhs_total + rhs_now
        tiled = jnp.concatenate([rhs_now] * NPAR + [jnp.zeros_like(rhs_now)], axis=0)
        normal = pick_left(same_source, tiled, NT)
        step = pick_right(gathered * normal, step_sel)
        grads_moved = jnp.zeros((cross, LANES), F32)
        for q in range(NPAR):
            grads_moved = grads_moved + step[:, q * rows : (q + 1) * rows] * cross_terms[q]
        grads = grads_before - jnp.where(live_knots, grads_moved, 0.0)
        both = jnp.concatenate(
            [jnp.where(lane_low, grads, 0.0), jnp.where(lane_low, 0.0, grads)], axis=0
        )
        windows = pick_left(window_hot, both)
        grad_mine[it] = windows[: n_sky * span2].reshape(n_sky, span2, LANES)
        rim_mine[it] = windows[n_sky * span2 :].reshape(2, HALO, LANES)
        @pl.when(t < n_tm - 1)
        def _():
            low_copy(it, s).start()

        @pl.when(t > 0)
        def _():
            high_copy(it, s).start()

        for i in range(1, n_sky):
            grad_copy(it, i).start()

        grad_all[it, s] = grad_mine[it, s]

        if it < ITERS - 1:
            base = base - source_term(step)
            on_base = against_params(base)
        if it == ITERS - 1:
            full_hot = onehot(
                iota((n_src, n_tm * cross), 0).astype(F32) == slots_all
            )
            padded = jnp.concatenate([rhs_total, jnp.zeros_like(rhs_total)], axis=0)
            normal_all = pick_right(padded, full_hot, NT)[:NPAR]
            steps = [
                jnp.sum(inverses[q] * normal_all, axis=0, keepdims=True) for q in range(NPAR)
            ]
            sources_out[...] = sources[...] + jnp.concatenate(steps, axis=0)

        for i in range(1, n_sky):
            grad_copy(it, i).wait_recv()

        @pl.when(from_low)
        def _():
            for i in range(n_sky):
                low_copy(it, i).wait_recv()

        @pl.when(from_high)
        def _():
            for i in range(n_sky):
                high_copy(it, i).wait_recv()

        packed = grad_all[it, 0]
        for i in range(1, n_sky):
            packed = packed + grad_all[it, i]
        low, high = rim_low[it, 0], rim_high[it, 0]
        for i in range(1, n_sky):
            low, high = low + rim_low[it, i], high + rim_high[it, i]
        packed = jnp.concatenate(
            [packed[:HALO] + low, packed[HALO : span2 - HALO], packed[span2 - HALO :] + high],
            axis=0,
        )
        grad = jnp.concatenate([packed, pltpu.roll(packed, LANES // 2, 1)], axis=0)
        grad = jnp.where(valid, grad, 0.0)
        delta = grad * inv_diag
        for sweep in range(SWEEPS - 1):
            near = jnp.concatenate(
                [pltpu.roll(delta, 1, 0), delta, pltpu.roll(delta, span - 1, 0)], axis=1
            )
            sums = pick_right(near, shift_hot)
            total = grad
            for b in range(n_band):
                total = total + bands[b] * sums[:, b * LANES : (b + 1) * LANES]
            delta = total * inv_diag
        knots_moved = knots_moved + delta[HALO : HALO + blocks]
        if it < ITERS - 1:
            knots_all[it + 1, s] = pack(knots_own + knots_moved)
            for i in range(1, n_sky):
                knots_copy(it + 1, i).start()
            for i in range(1, n_sky):
                knots_copy(it + 1, i).wait_recv()

    shape = (LANES, knots_here)
    c, d = iota(shape, 0), iota(shape, 1)
    own = (iota((blocks, knots_here), 1) >> 4) == iota((blocks, knots_here), 0)
    for a in range(NAX):
        unfold = onehot(jnp.logical_and((c >> 4) == a, (c & 15) == (d & 15)))
        line = jnp.where(own, pick_right(knots_moved, unfold), 0.0)
        attitude_out[a] = attitude[a] + jnp.sum(line, axis=0, keepdims=True)

    for it in range(ITERS):
        for i in range(1, n_sky):
            knots_copy(it, i).wait_send()
            grad_copy(it, i).wait_send()
        for i in range(1, n_tm):
            rhs_copy(it, i).wait_send()

        @pl.when(t < n_tm - 1)
        def _():
            low_copy(it, s).wait_send()

        @pl.when(t > 0)
        def _():
            high_copy(it, s).wait_send()

    @pl.when(has_right)
    def _():
        edge_copy(0).wait_send()

    @pl.when(has_left)
    def _():
        edge_copy(1).wait_send()


def finish(sources_in, attitude_in, sources_out, attitude_out):
    sources_out[...] = sources_in[...]
    attitude_out[...] = attitude_in[...]


def per_device(
    observed,
    att_partials,
    src_partials,
    src_slot,
    knot_block,
    live_count,
    sources,
    inverses,
    attitude,
    band_coef,
    extra_diag,
    band_offsets,
):
    n_sky, n_tm = lax.axis_size("sky"), lax.axis_size("tm")
    blocks = attitude.shape[2] // BLOCK_KNOTS
    span2 = (blocks + 2 * HALO) // 2
    vmem = pl.BlockSpec(memory_space=pltpu.VMEM)
    smem = pl.BlockSpec(memory_space=pltpu.SMEM)
    dma = pltpu.SemaphoreType.DMA
    results = pl.pallas_call(
        functools.partial(kernel, n_sky, n_tm),
        out_shape=(
            jax.ShapeDtypeStruct(sources.shape, F32),
            jax.ShapeDtypeStruct(attitude.shape, F32),
        ),
        in_specs=[vmem] * 5 + [smem] + [vmem] * 5 + [smem],
        out_specs=(vmem, vmem),
        scratch_shapes=[
            pltpu.VMEM((ITERS, n_sky, blocks // 2, LANES), F32),
            pltpu.VMEM((ITERS, n_tm, 8, src_slot.shape[0]), F32),
            pltpu.VMEM((ITERS, n_sky, span2, LANES), F32),
            pltpu.VMEM((ITERS, 2, HALO, LANES), F32),
            pltpu.VMEM((ITERS, n_sky, span2, LANES), F32),
            pltpu.VMEM((ITERS, n_sky, HALO, LANES), F32),
            pltpu.VMEM((ITERS, n_sky, HALO, LANES), F32),
            pltpu.VMEM((2, 16, LANES), F32),
            pltpu.VMEM((2, 16, LANES), F32),
            dma((ITERS, n_sky)),
            dma((ITERS, n_sky)),
            dma((ITERS, n_tm)),
            dma((ITERS, n_tm)),
            dma((ITERS, n_sky)),
            dma((ITERS, n_sky)),
            dma((ITERS, 2)),
            dma((ITERS, n_sky)),
            dma((ITERS, n_sky)),
            dma((2,)),
            dma((2,)),
        ],
        compiler_params=pltpu.CompilerParams(collective_id=0, has_side_effects=True),
    )(
        observed,
        att_partials,
        src_partials,
        src_slot[None, :],
        knot_block[None, :],
        live_count,
        sources,
        inverses,
        attitude,
        band_coef,
        extra_diag,
        band_offsets,
    )
    return pl.pallas_call(
        finish,
        out_shape=(
            jax.ShapeDtypeStruct(sources.shape, F32),
            jax.ShapeDtypeStruct(attitude.shape, F32),
        ),
        in_specs=[vmem] * 2,
        out_specs=(vmem, vmem),
    )(*results)


def solution(mesh):
    placed = (
        P(("sky", "tm"), None),
        P(None, ("sky", "tm"), None),
        P(None, ("sky", "tm"), None),
        P(("sky", "tm")),
        P(("sky", "tm")),
        P(("sky", "tm")),
        P(None, "sky"),
        P(None, None, "sky"),
        P(None, "tm", "sky"),
        P(None, None, "tm", "sky"),
        P(None, "tm", "sky"),
        P(),
    )
    return jax.shard_map(
        per_device,
        mesh=mesh,
        in_specs=placed,
        out_specs=(P(None, "sky"), P(None, "tm", "sky")),
        check_vma=False,
    )
```
